32 devices in a mesh: dp: 4 (over x, core), tensor: 8 (over z, y).
Axes of the slice: x: 2, y: 2, z: 4, core: 2. Of those that a mesh axis runs over, the one named last changes fastest.
Arguments:
- tokens: bfloat16 [768, 4096], P('dp', 'tensor'), may hold values from -6 to 6
- tangents: bfloat16 [768, 4096], P('dp', 'tensor'), may hold values from -6 to 6
- probes: bfloat16 [768, 4096], P('dp', 'tensor'), may hold values from -0.09375 to 0.09375
- w_gate: bfloat16 [4096, 14336], P('dp', 'tensor'), may hold values from -0.09375 to 0.09375
- w_up: bfloat16 [4096, 14336], P('dp', 'tensor'), may hold values from -0.09375 to 0.09375
- w_down: bfloat16 [14336, 4096], P('tensor'), may hold values from -3 to 3
Outputs:
- grad_gate: float32 [4096, 14336], P('dp', 'tensor')
- grad_up: float32 [4096, 14336], P('dp', 'tensor')
- projection: float32 [768], P('dp')
The draws below stay inside these ranges and needn't reach their ends.
All inputs are finite; a program needn't handle non-finite values.
Results may differ from the reference program's by a relative error of at most 0.019.
Values may be sent and summed in bfloat16 or wider, within the bound.
A program may use at most 128 MiB of HBM per device.

```python
import jax
import jax.numpy as jnp
from jax import lax

D = 4096
FF = 14336
TOK_DEV = 192
TOKENS = 768
N_DP = 4


def draw_w_down(key, part):
    base = jax.random.fold_in(key, 7)
    key_entry = jax.random.fold_in(base, 1)
    key_scale = jax.random.fold_in(base, 2)
    position = jnp.arange(FF, dtype=jnp.float32)[:, None] / FF
    jitter = jax.random.uniform(key_scale, (FF, 1), jnp.float32)
    row_scale = 0.3 * jnp.exp(jnp.log(10.0) * (0.5 * position + 0.5 * jitter))
    entries = jax.random.truncated_normal(key_entry, -4.0, 4.0, (FF, D), jnp.float32)
    return (entries * row_scale / jnp.sqrt(jnp.float32(FF))).astype(jnp.bfloat16)


def with_spikes(drawn, key, source, target, shards_of, factor):
    owner, partner = [(jnp.arange(drawn.shape[axis_at]) // (drawn.shape[axis_at] // shards_of)).reshape([-1 if axis == axis_at else 1 for axis in range(drawn.ndim)]) for axis_at in (source, target)]
    chosen = jax.random.permutation(key, shards_of)[partner]
    strong = (owner == chosen) | (owner == (partner + shards_of // 2) % shards_of)
    return jnp.where(strong, factor * drawn, drawn)


def block_levels(rng, shape, cuts, least, largest):
    loudness, own = 1.0, jax.random.fold_in(rng, 6)
    for axis_at, shards_of in cuts:
        heights = jnp.exp(jax.random.uniform(jax.random.fold_in(own, axis_at), (shards_of,), jnp.float32, least / len(cuts), largest / len(cuts)))
        loudness = loudness * jnp.repeat(heights, shape[axis_at] // shards_of).reshape([-1 if axis == axis_at else 1 for axis in range(len(shape))])
    return loudness


def normal_values(rng, shape, spread, reach, pieces=(), kind=jnp.bfloat16):
    values = jax.random.normal(rng, shape, jnp.float32) * spread
    if len(pieces) > 0:
        values = block_levels(rng, shape, pieces, -0.22, 0.18) * values
    return jnp.clip(values, min=-reach, max=reach).astype(kind)


def gaussian_with(rng, dims, deviation, most, cuts, heavy, kind=jnp.bfloat16):
    values = deviation * jax.random.normal(rng, dims, jnp.float32)
    if cuts:
        values = values * block_levels(rng, dims, cuts, -0.22, 0.18)
    return jnp.clip(with_spikes(values, jax.random.fold_in(rng, 3), *heavy), -most, most).astype(kind)


def setup_inputs(seed: int = 0) -> dict:
    splits = jax.random.split(jax.random.key(seed), 7)
    tokens = gaussian_with(splits[0], (TOKENS, D), 1.0, 6.0, ((0, 4), (1, 8)), (0, 1, 8, 2.0))
    tangents = normal_values(splits[1], (TOKENS, D), 1.0, 6.0, ((0, 4), (1, 8)))
    probes = normal_values(splits[2], (TOKENS, D), D ** -0.5, 0.09375, ((0, 4), (1, 8)))
    w_gate = normal_values(splits[3], (D, FF), D ** -0.5, 0.09375, ((0, 4), (1, 8)))
    w_up = normal_values(splits[4], (D, FF), D ** -0.5, 0.09375, ((0, 4), (1, 8)))
    w_down = draw_w_down(jax.random.fold_in(splits[6], 71), 0)
    return dict(tokens=tokens, tangents=tangents, probes=probes, w_gate=w_gate, w_up=w_up, w_down=w_down)


def reference(tokens, tangents, probes, w_gate, w_up, w_down):
    gate_val = jnp.dot(tokens, w_gate, preferred_element_type=jnp.float32)
    up_val = jnp.dot(tokens, w_up, preferred_element_type=jnp.float32)
    gate_dot = jnp.dot(tangents, w_gate, preferred_element_type=jnp.float32)
    up_dot = jnp.dot(tangents, w_up, preferred_element_type=jnp.float32)
    sigmoid_gate = jax.nn.sigmoid(gate_val)
    silu_val = gate_val * sigmoid_gate
    slope = sigmoid_gate * (1.0 + gate_val * (1.0 - sigmoid_gate))
    bend = sigmoid_gate * (1.0 - sigmoid_gate) * (2.0 + gate_val * (1.0 - 2.0 * sigmoid_gate))
    hidden_dot = slope * gate_dot * up_val + silu_val * up_dot
    readout = jnp.dot(probes, w_down.T, preferred_element_type=jnp.float32)
    projection = jnp.sum(hidden_dot * readout, axis=1)
    weight = 2.0 * projection[:, None] * readout
    g_gate = (weight * (bend * gate_dot * up_val + slope * up_dot)).astype(jnp.bfloat16)
    g_gate_dot = (weight * slope * up_val).astype(jnp.bfloat16)
    g_up = (weight * slope * gate_dot).astype(jnp.bfloat16)
    g_up_dot = (weight * silu_val).astype(jnp.bfloat16)

    def block_sum(carry, index):
        offset = (index * TOK_DEV).astype(jnp.int32)

        def rows_of(array):
            return lax.dynamic_slice_in_dim(array, offset, TOK_DEV, 0)

        inputs = jnp.concatenate([rows_of(tokens), rows_of(tangents)], axis=0)
        cot_gate = jnp.concatenate([rows_of(g_gate), rows_of(g_gate_dot)], axis=0)
        cot_up = jnp.concatenate([rows_of(g_up), rows_of(g_up_dot)], axis=0)
        part_gate = jnp.dot(inputs.T, cot_gate, preferred_element_type=jnp.float32).astype(jnp.bfloat16)
        part_up = jnp.dot(inputs.T, cot_up, preferred_element_type=jnp.float32).astype(jnp.bfloat16)
        part_gate, part_up = lax.optimization_barrier((part_gate, part_up))
        return (carry[0] + part_gate.astype(jnp.float32), carry[1] + part_up.astype(jnp.float32)), None

    zero_init = jnp.zeros((D, FF), jnp.float32)
    (grad_gate, grad_up), unused = lax.scan(block_sum, (zero_init, zero_init), jnp.arange(N_DP, dtype=jnp.int32))
    return grad_gate, grad_up, projection
```

```python
import functools

import jax
import jax.numpy as jnp
from jax import lax
from jax.sharding import PartitionSpec as P

CORES = 2


def body(n_dp, n_tensor, pieces, tokens, tangents, probes, w_gate, w_up, w_down):
    chips = n_dp // CORES
    me = lax.axis_index("dp")
    rows = tokens.shape[0]
    depth, hidden = w_gate.shape
    f32, bf16 = jnp.float32, jnp.bfloat16

    def shift(value, step, flip):
        pairs = []
        for at in range(n_dp):
            chip, core = at // CORES, at % CORES
            pairs.append((((chip + step) % chips) * CORES + (core ^ flip), at))
        return lax.ppermute(value, "dp", pairs)

    def owner(step, flip):
        return ((me // CORES + step) % chips) * CORES + ((me % CORES) ^ flip)

    both = jnp.stack([tokens, tangents], axis=0)
    full = lax.all_gather(both, "tensor", axis=2, tiled=True)
    full_probe = lax.all_gather(probes, "tensor", axis=1, tiled=True)

    def columns(at):
        return lax.dynamic_slice_in_dim(full, at * depth, depth, 2)

    blocks = [[None] * chips for _ in range(CORES)]
    for flip in range(CORES):
        for step in range(chips):
            if step == 0 and flip == 0:
                blocks[0][0] = columns(me)
            else:
                blocks[flip][step] = shift(columns(owner(-step, flip)), step, flip)
    own = jnp.stack(blocks[0], axis=1)
    far = jnp.stack(blocks[1], axis=1)
    own_rows = own.reshape(-1, depth)
    far_rows = far.reshape(-1, depth)

    readout = lax.dot_general(
        full_probe, w_down, (((1,), (1,)), ((), ())), preferred_element_type=f32
    )

    width = hidden // pieces
    projection = jnp.zeros((rows,), f32)
    gathered = []
    for piece in range(pieces):
        cut = slice(piece * width, (piece + 1) * width)
        wg, wu = w_gate[:, cut], w_up[:, cut]

        def partial(left, weight):
            return jnp.dot(left, weight, preferred_element_type=f32).reshape(2, chips, rows, width)

        sums = []
        for weight in (wg, wu):
            there = shift(partial(far_rows, weight).astype(bf16), 0, 1)
            here = partial(own_rows, weight) + there.astype(f32)
            total = here[:, 0]
            for step in range(1, chips):
                total = total + shift(here[:, step].astype(bf16), -step, 0).astype(f32)
            sums.append(total)
        gate_val, gate_dot = sums[0][0], sums[0][1]
        up_val, up_dot = sums[1][0], sums[1][1]
        sg = jax.nn.sigmoid(gate_val)
        silu_val = gate_val * sg
        slope = sg * (1.0 + gate_val * (1.0 - sg))
        bend = sg * (1.0 - sg) * (2.0 + gate_val * (1.0 - 2.0 * sg))
        out = readout[:, cut]
        hidden_dot = slope * gate_dot * up_val + silu_val * up_dot
        projection = projection + jnp.sum(hidden_dot * out, axis=1)
        cot = jnp.stack(
            [
                out * (bend * gate_dot * up_val + slope * up_dot),
                out * slope * up_val,
                out * slope * gate_dot,
                out * silu_val,
            ],
            axis=0,
        ).astype(bf16)
        mine = [cot] + [shift(cot, step, 0) for step in range(1, chips)]
        partner = [shift(value, 0, 1) for value in mine]
        gathered.append(jnp.stack(mine + partner, axis=1))

    bit = 1
    while bit < n_tensor:
        pairs = [(at ^ bit, at) for at in range(n_tensor)]
        projection = projection + lax.ppermute(projection, "tensor", pairs)
        bit *= 2
    factor = jnp.stack(
        [
            (projection if step == 0 and flip == 0 else shift(projection, step, flip))
            for flip in range(CORES)
            for step in range(chips)
        ]
    )
    scaled = jnp.concatenate([own, far], axis=1).astype(f32) * (2.0 * factor)[None, :, :, None]
    scaled = scaled.astype(bf16).reshape(-1, depth)

    grads = ([], [])
    for block in gathered:
        flat = block.reshape(2, -1, width)
        for at in range(2):
            grads[at].append(
                lax.dot_general(
                    scaled, flat[at], (((0,), (0,)), ((), ())), preferred_element_type=f32
                )
            )
    return (
        jnp.concatenate(grads[0], axis=1),
        jnp.concatenate(grads[1], axis=1),
        projection,
    )


def solution(mesh):
    n_dp, n_tensor = mesh.shape["dp"], mesh.shape["tensor"]
    placed = (P("dp", "tensor"),) * 5 + (P("tensor", None),)
    return jax.shard_map(
        functools.partial(body, n_dp, n_tensor, 2),
        mesh=mesh,
        in_specs=placed,
        out_specs=(P("dp", "tensor"), P("dp", "tensor"), P("dp")),
        check_vma=False,
    )
```

```python
import functools

import jax
import jax.numpy as jnp
from jax import lax
from jax.sharding import PartitionSpec as P

CORES = 2
PAIR = 2


def body(n_dp, n_tensor, pieces, tokens, tangents, probes, w_gate, w_up, w_down):
    chips = n_dp // CORES
    me = lax.axis_index("dp")
    rows = tokens.shape[0]
    depth, hidden = w_gate.shape
    f32, bf16 = jnp.float32, jnp.bfloat16

    def shift(value, step, flip):
        pairs = []
        for at in range(n_dp):
            chip, core = at // CORES, at % CORES
            pairs.append((((chip + step) % chips) * CORES + (core ^ flip), at))
        return lax.ppermute(value, "dp", pairs)

    def owner(step, flip):
        chip = lax.rem(lax.div(me, CORES) + step % chips, chips)
        return chip * CORES + (lax.rem(me, CORES) ^ flip)

    both = jnp.stack([tokens, tangents], axis=0)
    there = lax.axis_index("tensor")
    line, side = lax.div(there, PAIR), lax.rem(there, PAIR)
    length = n_tensor // PAIR

    def swap(value, lines):
        pairs = [(at ^ 1, at) for at in range(n_tensor) if at // PAIR in lines]
        return lax.ppermute(value, "tensor", pairs)

    def hop(value, step, lines):
        pairs = [(at - step * PAIR, at) for at in range(n_tensor) if at // PAIR in lines]
        return lax.ppermute(value, "tensor", pairs)

    def gather(value):
        found = [[value, swap(value, range(length))]]
        up, down = [], []
        rise = fall = value
        for far in range(1, length):
            higher, lower = range(far, length), range(length - far)
            rise = hop(rise, 1, higher)
            fall = hop(fall, -1, lower)
            up.append([rise, swap(rise, higher)])
            down.append([fall, swap(fall, lower)])
        for far in range(1, length):
            below, above = up[far - 1], down[length - far - 1]
            found.append([jnp.where(line >= far, below[k], above[k]) for k in range(PAIR)])
        blocks = jnp.stack([block for pair in found for block in pair])
        return blocks, rise

    def place(at):
        far = lax.rem(line + length - lax.div(at, PAIR), length)
        return far * PAIR + (side ^ lax.rem(at, PAIR))

    def take(blocks, first, count):
        picked = [
            lax.dynamic_index_in_dim(
                blocks, place(jnp.int32(first + k)), 0, keepdims=False, allow_negative_indices=False
            )
            for k in range(count)
        ]
        return jnp.concatenate(picked, axis=-1)

    full, last = gather(both)
    probes, last = lax.optimization_barrier((probes, last))
    full_probe = take(gather(probes)[0], 0, n_tensor)
    per = n_tensor // n_dp

    def columns(at):
        return take(full, at * per, per)

    blocks = [[None] * chips for _ in range(CORES)]
    for flip in range(CORES):
        for step in range(chips):
            if step == 0 and flip == 0:
                blocks[0][0] = columns(me)
            else:
                blocks[flip][step] = shift(columns(owner(-step, flip)), step, flip)
    own = jnp.stack(blocks[0], axis=1)
    far = jnp.stack(blocks[1], axis=1)
    own_rows = own.reshape(-1, depth)
    far_rows = far.reshape(-1, depth)

    readout = lax.dot_general(
        full_probe, w_down, (((1,), (1,)), ((), ())), preferred_element_type=f32
    )

    width = hidden // pieces
    projection = jnp.zeros((rows,), f32)
    gathered = []
    for piece in range(pieces):
        cut = slice(piece * width, (piece + 1) * width)
        wg, wu = w_gate[:, cut], w_up[:, cut]

        def partial(left, weight):
            return jnp.dot(left, weight, preferred_element_type=f32).reshape(2, chips, rows, width)

        sums = []
        for weight in (wg, wu):
            there = shift(partial(far_rows, weight).astype(bf16), 0, 1)
            here = partial(own_rows, weight) + there.astype(f32)
            total = here[:, 0]
            for step in range(1, chips):
                total = total + shift(here[:, step].astype(bf16), -step, 0).astype(f32)
            sums.append(total)
        gate_val, gate_dot = sums[0][0], sums[0][1]
        up_val, up_dot = sums[1][0], sums[1][1]
        sg = jax.nn.sigmoid(gate_val)
        silu_val = gate_val * sg
        slope = sg * (1.0 + gate_val * (1.0 - sg))
        bend = sg * (1.0 - sg) * (2.0 + gate_val * (1.0 - 2.0 * sg))
        out = readout[:, cut]
        hidden_dot = slope * gate_dot * up_val + silu_val * up_dot
        projection = projection + jnp.sum(hidden_dot * out, axis=1)
        cot = jnp.stack(
            [
                out * (bend * gate_dot * up_val + slope * up_dot),
                out * slope * up_val,
                out * slope * gate_dot,
                out * silu_val,
            ],
            axis=0,
        ).astype(bf16)
        mine = [cot] + [shift(cot, step, 0) for step in range(1, chips)]
        partner = [shift(value, 0, 1) for value in mine]
        gathered.append(jnp.stack(mine + partner, axis=1))

    bit = 1
    while bit < n_tensor:
        pairs = [(at ^ bit, at) for at in range(n_tensor)]
        projection = projection + lax.ppermute(projection, "tensor", pairs)
        bit *= 2
    factor = jnp.stack(
        [
            (projection if step == 0 and flip == 0 else shift(projection, step, flip))
            for flip in range(CORES)
            for step in range(chips)
        ]
    )
    scaled = jnp.concatenate([own, far], axis=1).astype(f32) * (2.0 * factor)[None, :, :, None]
    scaled = scaled.astype(bf16).reshape(-1, depth)

    grads = []
    for at in range(2):
        flat = jnp.concatenate([block[2 * at : 2 * at + 2] for block in gathered], axis=3)
        flat = flat.reshape(-1, hidden)
        grads.append(
            lax.dot_general(scaled, flat, (((0,), (0,)), ((), ())), preferred_element_type=f32)
        )
    return (grads[0], grads[1], projection)


def solution(mesh):
    n_dp, n_tensor = mesh.shape["dp"], mesh.shape["tensor"]
    placed = (P("dp", "tensor"),) * 5 + (P("tensor", None),)
    return jax.shard_map(
        functools.partial(body, n_dp, n_tensor, 2),
        mesh=mesh,
        in_specs=placed,
        out_specs=(P("dp", "tensor"), P("dp", "tensor"), P("dp")),
        check_vma=False,
    )
```

```python
import functools

import jax
import jax.numpy as jnp
from jax import lax
from jax.experimental import pallas as pl
from jax.experimental.pallas import tpu as pltpu
from jax.sharding import PartitionSpec as P

CORES = 2
PAIR = 2
MESH = pl.DeviceIdType.MESH


def gather_kernel(
    n_dp, n_tensor, both, probes, spread, full_probe, full, sent, landed, passed, arrived, local
):
    chips, per, length = n_dp // CORES, n_tensor // n_dp, n_tensor // PAIR
    wide = both.shape[2]
    me, there = lax.axis_index("dp"), lax.axis_index("tensor")
    line, side = lax.div(there, PAIR), lax.rem(there, PAIR)
    chip, core = lax.div(me, CORES), lax.rem(me, CORES)
    mate, above, below = line * PAIR + 1 - side, there + PAIR, there - PAIR

    barrier = pltpu.get_barrier_semaphore()

    def greet(where):
        pl.semaphore_signal(barrier, inc=1, device_id=where, device_id_type=MESH)

    greet({"tensor": mate})
    for step in range(1, n_dp):
        greet({"dp": lax.rem(me + step, n_dp)})
    pl.when(line < length - 1)(lambda: greet({"tensor": above}))
    pl.when(line > 0)(lambda: greet({"tensor": below}))
    ends = (line < length - 1).astype(jnp.int32) + (line > 0).astype(jnp.int32)
    pl.semaphore_wait(barrier, n_dp + ends)

    def columns(at):
        return pl.ds(pl.multiple_of(at * wide, 128), wide)

    def slot_of(stream, slot):
        return full.at[slot] if stream == 0 else full_probe.at[:, columns(slot)]

    def copy(stream, slot, way, source=None):
        where = (mate, above, below)[way]
        return pltpu.make_async_remote_copy(
            src_ref=slot_of(stream, slot) if source is None else source,
            dst_ref=slot_of(stream, slot),
            send_sem=sent.at[stream, slot, way],
            recv_sem=landed.at[stream, slot],
            device_id={"tensor": where},
            device_id_type=MESH,
        )

    def exchange(slot):
        owner, part = lax.div(slot, per), lax.rem(slot, per)
        step = lax.rem(chip - lax.div(owner, CORES) + chips, chips)
        flip = core ^ lax.rem(owner, CORES)
        away = pltpu.make_async_remote_copy(
            src_ref=full.at[slot],
            dst_ref=spread.at[flip, :, step, :, columns(part)],
            send_sem=passed.at[slot],
            recv_sem=arrived.at[flip, step, part],
            device_id={"dp": owner},
            device_id_type=MESH,
        )
        stay = pltpu.make_async_copy(
            full.at[slot], spread.at[0, :, 0, :, columns(part)], passed.at[slot]
        )
        return owner, away, stay

    def start_exchange(slot):
        owner, away, stay = exchange(slot)
        pl.when(owner != me)(away.start)
        pl.when(owner == me)(stay.start)

    def finish_exchange(slot):
        owner, away, stay = exchange(slot)
        pl.when(owner != me)(away.wait_send)
        pl.when(owner == me)(stay.wait)

    def relay(stream, far, final):
        for sign, way, goes in ((-1, 1, line < length - 1), (1, 2, line > 0)):
            at = line + sign * far
            slot = at * PAIR + side

            def run(slot=slot, way=way, goes=goes):
                if final:
                    pl.when(goes)(copy(stream, slot, way).wait_send)
                    copy(stream, slot, 0).wait_send()
                else:
                    copy(stream, slot, way).wait_recv()
                    pl.when(goes)(copy(stream, slot, way).start)
                    copy(stream, slot, 0).start()
                    if stream == 0:
                        start_exchange(slot)

            pl.when((at >= 0) & (at < length))(run)

    def across(stream, far):
        for sign in (-1, 1) if far else (1,):
            at = line + sign * far
            slot = at * PAIR + 1 - side

            def run(slot=slot):
                copy(stream, slot, 0).wait_recv()
                if stream == 0:
                    start_exchange(slot)

            pl.when((at >= 0) & (at < length))(run)

    holds = []
    for stream, source in ((0, both), (1, probes)):
        hold = pltpu.make_async_copy(source, slot_of(stream, there), local.at[stream])
        hold.start()
        holds.append(hold)
        pl.when(line < length - 1)(copy(stream, there, 1, source).start)
        pl.when(line > 0)(copy(stream, there, 2, source).start)
        copy(stream, there, 0, source).start()
        hold.wait()
        if stream == 0:
            start_exchange(there)
        for far in range(1, length):
            relay(stream, far, False)
            across(stream, far - 1)
        across(stream, length - 1)

    for stream, source in ((0, both), (1, probes)):
        pl.when(line < length - 1)(copy(stream, there, 1, source).wait_send)
        pl.when(line > 0)(copy(stream, there, 2, source).wait_send)
        copy(stream, there, 0, source).wait_send()
        for far in range(1, length):
            relay(stream, far, True)
    for slot in range(n_tensor):
        finish_exchange(jnp.int32(slot))
    for flip in range(CORES):
        for step in range(chips):
            for part in range(per):
                if flip == 0 and step == 0:
                    continue
                where = spread.at[flip, :, step, :, pl.ds(part * wide, wide)]
                pltpu.make_async_remote_copy(
                    src_ref=where,
                    dst_ref=where,
                    send_sem=passed.at[0],
                    recv_sem=arrived.at[flip, step, part],
                    device_id={"tensor": mate},
                    device_id_type=MESH,
                ).wait_recv()


def body(n_dp, n_tensor, pieces, tokens, tangents, probes, w_gate, w_up, w_down):
    chips = n_dp // CORES
    rows = tokens.shape[0]
    depth, hidden = w_gate.shape
    f32, bf16 = jnp.float32, jnp.bfloat16

    def shift(value, step, flip):
        pairs = []
        for at in range(n_dp):
            chip, core = at // CORES, at % CORES
            pairs.append((((chip + step) % chips) * CORES + (core ^ flip), at))
        return lax.ppermute(value, "dp", pairs)

    both = jnp.stack([tokens, tangents], axis=0)
    spread, full_probe = pl.pallas_call(
        functools.partial(gather_kernel, n_dp, n_tensor),
        out_shape=(
            jax.ShapeDtypeStruct((CORES, 2, chips, rows, depth), bf16),
            jax.ShapeDtypeStruct((rows, n_tensor * probes.shape[1]), bf16),
        ),
        in_specs=[pl.BlockSpec(memory_space=pltpu.VMEM)] * 2,
        out_specs=[pl.BlockSpec(memory_space=pltpu.VMEM)] * 2,
        scratch_shapes=[
            pltpu.VMEM((n_tensor,) + both.shape, bf16),
            pltpu.SemaphoreType.DMA((2, n_tensor, 3)),
            pltpu.SemaphoreType.DMA((2, n_tensor)),
            pltpu.SemaphoreType.DMA((n_tensor,)),
            pltpu.SemaphoreType.DMA((CORES, chips, n_tensor // n_dp)),
            pltpu.SemaphoreType.DMA((2,)),
        ],
        compiler_params=pltpu.CompilerParams(collective_id=0, has_side_effects=True),
    )(both, probes)
    own, far = spread[0], spread[1]
    own_rows = own.reshape(-1, depth)
    far_rows = far.reshape(-1, depth)

    readout = lax.dot_general(
        full_probe, w_down, (((1,), (1,)), ((), ())), preferred_element_type=f32
    )

    width = hidden // pieces
    projection = jnp.zeros((rows,), f32)
    mines = []
    for piece in range(pieces):
        cut = slice(piece * width, (piece + 1) * width)
        wg, wu = w_gate[:, cut], w_up[:, cut]

        def partial(left, weight):
            return jnp.dot(left, weight, preferred_element_type=f32).reshape(2, chips, rows, width)

        sums = []
        for weight in (wg, wu):
            there = shift(partial(far_rows, weight).astype(bf16), 0, 1)
            here = partial(own_rows, weight) + there.astype(f32)
            total = here[:, 0]
            for step in range(1, chips):
                total = total + shift(here[:, step].astype(bf16), -step, 0).astype(f32)
            sums.append(total)
        gate_val, gate_dot = sums[0][0], sums[0][1]
        up_val, up_dot = sums[1][0], sums[1][1]
        sg = jax.nn.sigmoid(gate_val)
        silu_val = gate_val * sg
        slope = sg * (1.0 + gate_val * (1.0 - sg))
        bend = sg * (1.0 - sg) * (2.0 + gate_val * (1.0 - 2.0 * sg))
        out = readout[:, cut]
        hidden_dot = slope * gate_dot * up_val + silu_val * up_dot
        projection = projection + jnp.sum(hidden_dot * out, axis=1)
        cot = jnp.stack(
            [
                out * (bend * gate_dot * up_val + slope * up_dot),
                out * slope * up_val,
                out * slope * gate_dot,
                out * silu_val,
            ],
            axis=0,
        ).astype(bf16)
        mines.append([cot] + [shift(cot, step, 0) for step in range(1, chips)])

    bit = 1
    while bit < n_tensor:
        pairs = [(at ^ bit, at) for at in range(n_tensor)]
        projection = projection + lax.ppermute(projection, "tensor", pairs)
        bit *= 2
    factor = jnp.stack(
        [
            (projection if step == 0 and flip == 0 else shift(projection, step, flip))
            for flip in range(CORES)
            for step in range(chips)
        ]
    )
    gathered = []
    for piece, mine in enumerate(mines):
        if piece == 0:
            mine[1], factor = lax.optimization_barrier((mine[1], factor))
        partner = [shift(value, 0, 1) for value in mine]
        gathered.append(jnp.stack(mine + partner, axis=1))
    scaled = jnp.concatenate([own, far], axis=1).astype(f32) * (2.0 * factor)[None, :, :, None]
    scaled = scaled.astype(bf16).reshape(-1, depth)

    grads = []
    for at in range(2):
        flat = jnp.concatenate([block[2 * at : 2 * at + 2] for block in gathered], axis=3)
        flat = flat.reshape(-1, hidden)
        grads.append(
            lax.dot_general(scaled, flat, (((0,), (0,)), ((), ())), preferred_element_type=f32)
        )
    return (grads[0], grads[1], projection)


def solution(mesh):
    n_dp, n_tensor = mesh.shape["dp"], mesh.shape["tensor"]
    placed = (P("dp", "tensor"),) * 5 + (P("tensor", None),)
    return jax.shard_map(
        functools.partial(body, n_dp, n_tensor, 2),
        mesh=mesh,
        in_specs=placed,
        out_specs=(P("dp", "tensor"), P("dp", "tensor"), P("dp")),
        check_vma=False,
    )
```
